32 devices in a mesh: seg: 8 (over z, x), head: 4 (over y, core).
Axes of the slice: x: 2, y: 2, z: 4, core: 2. Of those that a mesh axis runs over, the one named last changes fastest.
Arguments:
- q_heads: bfloat16 [6144, 2048], P('seg', 'head'), may hold values from -6 to 6
- k_heads: bfloat16 [6144, 2048], P('seg', 'head'), may hold values from -6 to 6
- v_heads: bfloat16 [6144, 2048], P('seg', 'head'), may hold values from -600 to 600
- log_decay: float32 [16, 6144], P('head', 'seg'), may hold values from -1 to 0
- parent: int32 [8], replicated, may hold values from -1 to 7, as said below
- norm_gain: float32 [2048], P('head'), may hold values from 0.1 to 1.9
- w_out: bfloat16 [2048, 6144], P('head'), may hold values from -0.125 to 0.125
Outputs:
- mixed: bfloat16 [6144, 6144], P(('seg', 'head'))
The draws below stay inside these ranges and needn't reach their ends.
Inputs may be any that keep to these rules, and one draw needn't show every extreme that they name: A segment's parent is a root or a segment whose parent is a root; the tree has three levels, and the third is never empty.
All inputs are finite; a program needn't handle non-finite values.
Results may differ from the reference program's by a relative error of at most 0.0051.
Values sent between devices are 32-bit elements; how exact they have to be, the bound alone decides.
A program may use at most 128 MiB of HBM per device.

```python
import math
import jax
import jax.numpy as jnp
from jax import lax

HID = 6144
DH = 128
SEGMENT_LENGTH = 768
HEAD_TOTAL = 16
FEAT = 2048
NSEG = 8
TOKEN_TOTAL = 6144


def draw_parent(key, part):
    key_order = jax.random.fold_in(key, 101)
    key_root = jax.random.fold_in(key, 102)
    key_middle = jax.random.fold_in(key, 103)
    rest = jax.random.permutation(key_order, NSEG - 1).astype(jnp.int32)
    order = jnp.concatenate([jnp.full((1,), NSEG - 1, jnp.int32), rest]).astype(jnp.int32)
    first = max(NSEG // 8, 1)
    second = first + max(NSEG * 3 // 8, 1)
    rank = jnp.arange(NSEG, dtype=jnp.int32)
    pick_root = jax.random.randint(key_root, (NSEG,), 0, first)
    pick_root = jnp.where(rank == first, 0, pick_root)
    pick_middle = jax.random.randint(key_middle, (NSEG,), first, second)
    pick_middle = jnp.where(rank == second, first, pick_middle)
    by_rank = jnp.where(rank < first, -1, jnp.where(rank < second, order[pick_root], order[pick_middle]))
    return jnp.zeros((NSEG,), jnp.int32).at[order].set(by_rank.astype(jnp.int32))


def draw_log_decay(key, part):
    key_fast = jax.random.fold_in(key, 201)
    key_slow = jax.random.fold_in(key, 202)
    key_quick = jax.random.fold_in(key, 203)
    key_segment = jax.random.fold_in(key, 204)
    key_rough = jax.random.fold_in(key, 205)
    key_spike_seed = jax.random.fold_in(key, 206)
    key_loss = jax.random.fold_in(key, 207)
    chain = 3.0 * SEGMENT_LENGTH
    share = 0.5
    fast = (jax.random.uniform(key_fast, (HEAD_TOTAL, 1, 1)) < share).astype(jnp.float32)
    slow_rate = jnp.exp(jax.random.uniform(key_slow, (HEAD_TOTAL, 1, 1), minval=math.log(0.05), maxval=math.log(0.5))) / chain
    quick_rate = jnp.exp(jax.random.uniform(key_quick, (HEAD_TOTAL, 1, 1), minval=math.log(1.0 / 50.0), maxval=math.log(1.0 / 30.0)))
    rate = fast * quick_rate + (1.0 - fast) * slow_rate
    segment_factor = jnp.exp(jax.random.uniform(key_segment, (HEAD_TOTAL, NSEG, 1), minval=math.log(0.5), maxval=0.0))
    rough = jax.random.uniform(key_rough, (HEAD_TOTAL, NSEG, SEGMENT_LENGTH), minval=0.5, maxval=1.5)
    stable_level = (rate * segment_factor * rough).reshape(HEAD_TOTAL, TOKEN_TOTAL)
    sudden_spike = jax.random.uniform(key_spike_seed, (HEAD_TOTAL, TOKEN_TOTAL)) < 1.0 / SEGMENT_LENGTH
    training_loss = jnp.log(jax.random.uniform(key_loss, (HEAD_TOTAL, TOKEN_TOTAL), minval=0.5, maxval=0.8))
    return (-stable_level + jnp.where(sudden_spike, training_loss, 0.0)).astype(jnp.float32)


def draw_v_heads(key, part):
    key_base = jax.random.fold_in(key, 301)
    key_row = jax.random.fold_in(key, 302)
    key_head = jax.random.fold_in(key, 303)
    base = jnp.clip(jax.random.normal(key_base, (TOKEN_TOTAL, FEAT)), -6.0, 6.0)
    row_scale = jnp.exp(jax.random.uniform(key_row, (TOKEN_TOTAL, 1), minval=0.0, maxval=math.log(10.0)))
    head_index = jnp.arange(FEAT) // DH
    rising = 3.0 ** (head_index.astype(jnp.float32) / max(HEAD_TOTAL - 1, 1))
    spread = jnp.exp(jax.random.uniform(key_head, (HEAD_TOTAL,), minval=0.0, maxval=math.log(3.3)))[head_index]
    return jnp.clip(base * row_scale * rising * spread, -600.0, 600.0).astype(jnp.bfloat16)


def level_of(key, dims, shards, least, top_value):
    def one(dim, parts):
        steps = jax.random.uniform(jax.random.fold_in(jax.random.fold_in(key, 6), dim), (parts,), jnp.float32, least / len(shards), top_value / len(shards))
        return jnp.repeat(jnp.exp(steps), dims[dim] // parts).reshape((-1,) + (1,) * (len(dims) - dim - 1))

    level = one(*shards[0])
    for cut in shards[1:]:
        level = level * one(*cut)
    return level


def noise(own_key, extent, scale, limit, pieces=(), held_as=jnp.bfloat16):
    loudness = level_of(own_key, extent, pieces, -0.22, 0.18) if pieces else 1.0
    values = jax.random.normal(own_key, extent, jnp.float32) * scale * loudness
    return jnp.minimum(jnp.maximum(values, -limit), limit).astype(held_as)


def setup_inputs(seed: int = 0) -> dict:
    keys = jax.random.split(jax.random.key(seed), 8)
    return {
        "q_heads": noise(keys[0], (TOKEN_TOTAL, FEAT), 1.0, 6.0, ((0, 8), (1, 4))),
        "k_heads": noise(keys[1], (TOKEN_TOTAL, FEAT), 1.0, 6.0, ((0, 8), (1, 4))),
        "v_heads": draw_v_heads(jax.random.fold_in(keys[7], 71), 0),
        "log_decay": draw_log_decay(jax.random.fold_in(keys[7], 71), 0),
        "parent": draw_parent(jax.random.fold_in(keys[7], 71), 0),
        "norm_gain": jnp.clip(1.0 + 0.18 * jax.random.normal(keys[5], (FEAT,), jnp.float32), 0.1, 1.9),
        "w_out": noise(keys[6], (FEAT, HID), FEAT ** -0.5, 0.125, ((0, 4),)),
    }


def segment_state(key_rows, values, decay_logs):
    running = jnp.cumsum(decay_logs, axis=1)
    segment_total = running[:, -1]
    key_weight = jnp.exp(segment_total[:, None] - running)
    weighted = key_rows.astype(jnp.float32) * key_weight.T[:, :, None]
    local_state = jnp.einsum('shd,she->hde', weighted, values.astype(jnp.float32), precision=lax.Precision.HIGHEST)
    return (running, local_state, segment_total)

def segment_output(queries, key_rows, values, running, prefix):
    length = queries.shape[0]
    scale = DH ** (-0.5)
    scores = jnp.einsum('thd,shd->hts', queries.astype(jnp.float32), key_rows.astype(jnp.float32), precision=lax.Precision.HIGHEST)
    row_index = lax.broadcasted_iota(jnp.int32, (length, length), 0)
    col_index = lax.broadcasted_iota(jnp.int32, (length, length), 1)
    causal = row_index >= col_index
    log_gap = running[:, :, None] - running[:, None, :]
    decay_factor = jnp.where(causal[None], jnp.exp(jnp.minimum(log_gap, 0.0)), 0.0)
    weights = (scores * scale * decay_factor).astype(jnp.bfloat16)
    within = jnp.einsum('hts,she->the', weights.astype(jnp.float32), values.astype(jnp.float32), precision=lax.Precision.HIGHEST)
    prefix_term = jnp.einsum('thd,hde->the', queries.astype(jnp.float32), prefix, precision=lax.Precision.HIGHEST) * jnp.exp(running).T[:, :, None]
    return prefix_term + within

def reference(q_heads, k_heads, v_heads, log_decay, parent, norm_gain, w_out):
    queries = q_heads.reshape(NSEG, SEGMENT_LENGTH, HEAD_TOTAL, DH)
    key_rows = k_heads.reshape(NSEG, SEGMENT_LENGTH, HEAD_TOTAL, DH)
    values = v_heads.reshape(NSEG, SEGMENT_LENGTH, HEAD_TOTAL, DH)
    decays = log_decay.reshape(HEAD_TOTAL, NSEG, SEGMENT_LENGTH).transpose(1, 0, 2)
    running, local_state, segment_total = lax.map(lambda items: segment_state(*items), (key_rows, values, decays))
    has_parent = parent >= 0
    parent_index = jnp.maximum(parent, 0).astype(jnp.int32)
    end_state = local_state
    prefix = jnp.zeros_like(local_state)
    for step_index in range(2):
        prefix = jnp.where(has_parent[:, None, None, None], end_state[parent_index], jnp.float32(0.0))
        end_state = jnp.exp(segment_total)[:, :, None, None] * prefix + local_state
    attention = lax.map(lambda items: segment_output(*items), (queries, key_rows, values, running, prefix))
    attention = attention.reshape(TOKEN_TOTAL, FEAT)
    squares = lax.optimization_barrier(jnp.sum(attention * attention, axis=1))
    inverse = 1.0 / jnp.sqrt(squares / FEAT + 1e-06)
    normed = (attention * inverse[:, None] * norm_gain[None, :]).astype(jnp.bfloat16)
    return jnp.dot(normed, w_out, preferred_element_type=jnp.float32).astype(jnp.bfloat16)
```

```python
import jax
import jax.numpy as jnp
from jax import lax
from jax.sharding import PartitionSpec as P


def ring_order(count):
    half = (count + 1) // 2
    return [2 * i if i < half else 2 * (count - 1 - i) + 1 for i in range(count)]


def doubled(array):
    return (array * 2.0).astype(jnp.bfloat16)


def per_device(q_heads, k_heads, v_heads, log_decay, parent, norm_gain, w_out):
    segment_len, features = q_heads.shape
    head_count = log_decay.shape[0]
    head_width = features // head_count
    hidden = w_out.shape[1]
    seg_count = lax.axis_size("seg")
    head_parts = lax.axis_size("head")
    chips = head_parts // 2
    own_index = lax.axis_index("seg")
    own_head = lax.axis_index("head")
    own_chip, own_core = own_head // 2, own_head % 2
    rows = segment_len // head_parts

    swap = [(i, i ^ 1) for i in range(head_parts)]

    def to_core(array):
        return lax.ppermute(array, "head", swap)

    def to_chip(array, step):
        perm = [(i, (i + 2 * step) % head_parts) for i in range(head_parts)]
        return lax.ppermute(array, "head", perm)

    order = ring_order(seg_count)
    forward = [(order[i], order[(i + 1) % seg_count]) for i in range(seg_count)]
    backward = [(b, a) for a, b in forward]
    half = (seg_count + 1) // 2
    own_place = jnp.where(
        own_index % 2 == 0, own_index // 2, seg_count - 1 - own_index // 2
    )

    def segment_at(place):
        place = (place + seg_count) % seg_count
        return jnp.where(place < half, 2 * place, 2 * (seg_count - 1 - place) + 1)

    gathered = hidden // 2
    shard = gathered // seg_count
    w_far = jnp.concatenate(
        [
            to_chip(
                lax.dynamic_slice_in_dim(w_out, own_index * shard, shard, axis=1).astype(jnp.float32),
                step,
            )
            for step in range(1, chips)
        ],
        axis=0,
    )
    w_mate = doubled(to_core(w_out.astype(jnp.float32)))
    gain_chip = jnp.concatenate([norm_gain, to_core(norm_gain)])
    gain_far = jnp.concatenate([to_chip(gain_chip, step) for step in range(1, chips)]) * 0.5
    gain_chip = gain_chip * jnp.repeat(jnp.array([1.0, 0.5], jnp.float32), norm_gain.shape[0])

    queries = q_heads.reshape(segment_len, head_count, head_width)
    key_rows = k_heads.reshape(segment_len, head_count, head_width)
    values = v_heads.reshape(segment_len, head_count, head_width)
    running = jnp.cumsum(log_decay, axis=1)
    segment_total = running[:, -1]
    key_weight = jnp.exp(segment_total[:, None] - running)
    weighted = key_rows.astype(jnp.float32) * key_weight.T[:, :, None]
    local_state = jnp.einsum(
        "shd,she->hde", weighted, values.astype(jnp.float32), precision=lax.Precision.HIGHEST
    )
    state_rows = head_count * head_width
    packed = jnp.concatenate(
        [
            local_state.reshape(state_rows, head_width),
            jnp.broadcast_to(segment_total[:, None], (head_count, head_width)),
        ],
        axis=0,
    )

    held = [(own_index, packed)]
    ahead = behind = packed
    for step in range(1, seg_count // 2 + 1):
        ahead = lax.ppermute(ahead, "seg", forward)
        held.append((segment_at(own_place - step), ahead))
        if step <= (seg_count - 1) // 2:
            behind = lax.ppermute(behind, "seg", backward)
            held.append((segment_at(own_place + step), behind))

    ring = [[(own_index, w_far)]]
    ahead_w = behind_w = w_far
    for step in range(1, seg_count // 2 + 1):
        if step == 2:
            ahead_w, behind_w, ahead, behind = lax.optimization_barrier(
                (ahead_w, behind_w, ahead, behind)
            )
        ahead_w = lax.ppermute(ahead_w, "seg", forward)
        arrived = [(segment_at(own_place - step), ahead_w)]
        if step <= (seg_count - 1) // 2:
            behind_w = lax.ppermute(behind_w, "seg", backward)
            arrived.append((segment_at(own_place + step), behind_w))
        ring.append(arrived)
    ring[0:2] = [ring[0] + ring[1]]

    scores = jnp.einsum("thd,shd->hts", queries, key_rows, preferred_element_type=jnp.float32)
    row_index = lax.broadcasted_iota(jnp.int32, (segment_len, segment_len), 0)
    col_index = lax.broadcasted_iota(jnp.int32, (segment_len, segment_len), 1)
    causal = row_index >= col_index
    log_gap = running[:, :, None] - running[:, None, :]
    decay_factor = jnp.where(causal[None], jnp.exp(jnp.minimum(log_gap, 0.0)), 0.0)
    weights = (scores * head_width ** (-0.5) * decay_factor).astype(jnp.bfloat16)
    within = jnp.einsum("hts,she->the", weights, values, preferred_element_type=jnp.float32)

    parent_id = parent[own_index]
    grand_id = jnp.where(parent_id >= 0, parent[jnp.maximum(parent_id, 0)], -1)
    parent_pack = sum(jnp.where(index == parent_id, pack, 0.0) for index, pack in held)
    grand_sum = sum(jnp.where(index == grand_id, pack[:state_rows], 0.0) for index, pack in held)
    shape = (head_count, head_width, head_width)
    prefix = jnp.exp(parent_pack[state_rows:])[:, None, :] * grand_sum.reshape(
        shape
    ) + parent_pack[:state_rows].reshape(shape)
    prefix_term = (
        jnp.einsum(
            "thd,hde->the", queries.astype(jnp.float32), prefix, precision=lax.Precision.HIGHEST
        )
        * jnp.exp(running).T[:, :, None]
    )
    attention = (prefix_term + within).reshape(segment_len, features)
    attention = attention.reshape(chips, 2, rows, features)

    def core_rows(array, core):
        return lax.dynamic_index_in_dim(array, core, axis=1, keepdims=False)

    mate = to_core(core_rows(attention, 1 - own_core))
    chip_rows = jnp.concatenate([core_rows(attention, own_core), mate], axis=2)

    def chip_block(array, step):
        return lax.dynamic_index_in_dim(array, (own_chip + step) % chips, axis=0, keepdims=False)

    def scaled(array, gain):
        return (array * gain[None, :]).astype(jnp.bfloat16)

    own_wide = chip_block(chip_rows, 0)
    away = [chip_block(chip_rows, step) for step in range(1, chips)]
    far_wide = jnp.concatenate([to_chip(block, step) for step, block in enumerate(away, 1)], axis=1)
    own_rows = scaled(own_wide, gain_chip)
    away_rows = scaled(jnp.concatenate(away, axis=0), gain_chip)
    far_rows = scaled(far_wide, gain_far)
    total_squares = jnp.sum(own_wide * own_wide, axis=1) + jnp.sum(far_wide * far_wide, axis=1)
    inverse = (1.0 / jnp.sqrt(total_squares / (features * head_parts) + 1e-06))[:, None]

    def multiply(left, right):
        return jnp.dot(left, right, preferred_element_type=jnp.float32)

    def chip_product(left, low, high):
        return multiply(left[:, :features], w_out[:, low:high]) + multiply(
            left[:, features:], w_mate[:, low:high]
        )

    cuts = 3
    width = (hidden - gathered) // cuts
    summed = []
    for cut in range(cuts):
        low = gathered + cut * width
        part = chip_product(away_rows, low, low + width)
        total = chip_product(own_rows, low, low + width)
        for step in range(1, chips):
            total = total + to_chip(part[(step - 1) * rows : step * rows], step)
        summed.append((total * inverse).astype(jnp.bfloat16))

    product = chip_product(own_rows, 0, gathered)
    left_own = [far_rows[:, 2 * features * i : 2 * features * i + features] for i in range(chips - 1)]
    left_mate = [far_rows[:, 2 * features * i + features : 2 * features * (i + 1)] for i in range(chips - 1)]
    left_own = jnp.concatenate(left_own, axis=1)
    left_mate = jnp.concatenate(left_mate, axis=1)
    placed = jnp.zeros((rows, gathered), jnp.float32)
    for arrived in ring:
        mine = jnp.concatenate([block for _, block in arrived], axis=1)
        other = to_core(mine)
        block = multiply(left_own, doubled(mine)) + multiply(left_mate, doubled(other))
        for place, (index, _) in enumerate(arrived):
            placed = lax.dynamic_update_slice_in_dim(
                placed, block[:, place * shard : (place + 1) * shard], index * shard, axis=1
            )
    first = ((product + placed) * inverse).astype(jnp.bfloat16)
    return jnp.concatenate([first] + summed, axis=1)


def solution(mesh):
    return jax.shard_map(
        per_device,
        mesh=mesh,
        in_specs=(
            P("seg", "head"),
            P("seg", "head"),
            P("seg", "head"),
            P("head", "seg"),
            P(),
            P("head"),
            P("head", None),
        ),
        out_specs=P(("seg", "head"), None),
        check_vma=False,
    )
```

```python
import jax
import jax.numpy as jnp
from jax import lax
from jax.sharding import PartitionSpec as P


def ring_order(count):
    half = (count + 1) // 2
    return [2 * i if i < half else 2 * (count - 1 - i) + 1 for i in range(count)]


def doubled(array):
    return (array * 2.0).astype(jnp.bfloat16)


def per_device(q_heads, k_heads, v_heads, log_decay, parent, norm_gain, w_out):
    segment_len, features = q_heads.shape
    head_count = log_decay.shape[0]
    head_width = features // head_count
    hidden = w_out.shape[1]
    seg_count = lax.axis_size("seg")
    head_parts = lax.axis_size("head")
    chips = head_parts // 2
    own_index = lax.axis_index("seg")
    own_head = lax.axis_index("head")
    own_chip, own_core = own_head // 2, own_head % 2
    rows = segment_len // head_parts

    swap = [(i, i ^ 1) for i in range(head_parts)]

    def to_core(array):
        return lax.ppermute(array, "head", swap)

    def to_chip(array, step):
        perm = [(i, (i + 2 * step) % head_parts) for i in range(head_parts)]
        return lax.ppermute(array, "head", perm)

    order = ring_order(seg_count)
    forward = [(order[i], order[(i + 1) % seg_count]) for i in range(seg_count)]
    backward = [(b, a) for a, b in forward]
    half = (seg_count + 1) // 2
    own_place = jnp.where(
        own_index % 2 == 0, own_index // 2, seg_count - 1 - own_index // 2
    )

    def segment_at(place):
        place = (place + seg_count) % seg_count
        return jnp.where(place < half, 2 * place, 2 * (seg_count - 1 - place) + 1)

    gathered = hidden // 2
    shard = gathered // seg_count
    w_piece = lax.dynamic_slice_in_dim(w_out, own_index * shard, shard, axis=1).astype(jnp.float32)
    w_piece, log_decay = lax.optimization_barrier((w_piece, log_decay))
    w_far = jnp.concatenate([to_chip(w_piece, step) for step in range(1, chips)], axis=0)
    gain_chip = jnp.concatenate([norm_gain, to_core(norm_gain)])
    gain_far = jnp.concatenate([to_chip(gain_chip, step) for step in range(1, chips)]) * 0.5
    gain_chip = gain_chip * jnp.repeat(jnp.array([1.0, 0.5], jnp.float32), norm_gain.shape[0])

    queries = q_heads.reshape(segment_len, head_count, head_width)
    key_rows = k_heads.reshape(segment_len, head_count, head_width)
    values = v_heads.reshape(segment_len, head_count, head_width)
    running = jnp.cumsum(log_decay, axis=1)
    segment_total = running[:, -1]
    key_weight = jnp.exp(segment_total[:, None] - running)
    weighted = key_rows.astype(jnp.float32) * key_weight.T[:, :, None]
    local_state = jnp.einsum(
        "shd,she->hde", weighted, values.astype(jnp.float32), precision=lax.Precision.HIGHEST
    )
    state_rows = head_count * head_width
    packed = jnp.concatenate(
        [
            local_state.reshape(state_rows, head_width),
            jnp.broadcast_to(segment_total[:, None], (head_count, head_width)),
        ],
        axis=0,
    )

    w_late, packed = lax.optimization_barrier((w_out, packed))
    w_mate = to_core(w_late[:, gathered:].astype(jnp.float32))
    w_mate_gathered = doubled(to_core(w_late[:, :gathered].astype(jnp.float32)))

    held = [(own_index, packed)]
    ahead = behind = packed
    for step in range(1, seg_count // 2 + 1):
        if step == 2:
            ahead, behind, w_far = lax.optimization_barrier((ahead, behind, w_far))
        ahead = lax.ppermute(ahead, "seg", forward)
        held.append((segment_at(own_place - step), ahead))
        if step <= (seg_count - 1) // 2:
            behind = lax.ppermute(behind, "seg", backward)
            held.append((segment_at(own_place + step), behind))

    ahead, behind, w_mate = lax.optimization_barrier((ahead, behind, w_mate))
    held[-2 if seg_count % 2 else -1] = (held[-2 if seg_count % 2 else -1][0], ahead)
    w_mate = doubled(w_mate)

    scores = jnp.einsum("thd,shd->hts", queries, key_rows, preferred_element_type=jnp.float32)
    row_index = lax.broadcasted_iota(jnp.int32, (segment_len, segment_len), 0)
    col_index = lax.broadcasted_iota(jnp.int32, (segment_len, segment_len), 1)
    causal = row_index >= col_index
    log_gap = running[:, :, None] - running[:, None, :]
    decay_factor = jnp.where(causal[None], jnp.exp(jnp.minimum(log_gap, 0.0)), 0.0)
    weights = (scores * head_width ** (-0.5) * decay_factor).astype(jnp.bfloat16)
    within = jnp.einsum("hts,she->the", weights, values, preferred_element_type=jnp.float32)

    parent_id = parent[own_index]
    grand_id = jnp.where(parent_id >= 0, parent[jnp.maximum(parent_id, 0)], -1)
    parent_pack = sum(jnp.where(index == parent_id, pack, 0.0) for index, pack in held)
    grand_sum = sum(jnp.where(index == grand_id, pack[:state_rows], 0.0) for index, pack in held)
    shape = (head_count, head_width, head_width)
    prefix = jnp.exp(parent_pack[state_rows:])[:, None, :] * grand_sum.reshape(
        shape
    ) + parent_pack[:state_rows].reshape(shape)
    prefix_term = (
        jnp.einsum(
            "thd,hde->the", queries.astype(jnp.float32), prefix, precision=lax.Precision.HIGHEST
        )
        * jnp.exp(running).T[:, :, None]
    )
    attention = (prefix_term + within).reshape(segment_len, features)
    attention, w_mate = lax.optimization_barrier((attention, w_mate))

    attention = attention.reshape(chips, 2, rows, features)

    def core_rows(array, core):
        return lax.dynamic_index_in_dim(array, core, axis=1, keepdims=False)

    mate = to_core(core_rows(attention, 1 - own_core))
    chip_rows = jnp.concatenate([core_rows(attention, own_core), mate], axis=2)

    def chip_block(array, step):
        return lax.dynamic_index_in_dim(array, (own_chip + step) % chips, axis=0, keepdims=False)

    def scaled(array, gain):
        return (array * gain[None, :]).astype(jnp.bfloat16)

    own_wide = chip_block(chip_rows, 0)
    away = [chip_block(chip_rows, step) for step in range(1, chips)]
    far_wide = jnp.concatenate([to_chip(block, step) for step, block in enumerate(away, 1)], axis=1)
    own_rows = scaled(own_wide, gain_chip)
    away_rows = scaled(jnp.concatenate(away, axis=0), gain_chip)
    far_rows = scaled(far_wide, gain_far)
    total_squares = jnp.sum(own_wide * own_wide, axis=1) + jnp.sum(far_wide * far_wide, axis=1)
    inverse = (1.0 / jnp.sqrt(total_squares / (features * head_parts) + 1e-06))[:, None]

    def multiply(left, right):
        return jnp.dot(left, right, preferred_element_type=jnp.float32)

    def chip_product(left, low, high):
        mate_block = (
            w_mate_gathered[:, low:high]
            if high <= gathered
            else w_mate[:, low - gathered : high - gathered]
        )
        return multiply(left[:, :features], w_out[:, low:high]) + multiply(
            left[:, features:], mate_block
        )

    cuts = 3
    width = (hidden - gathered) // cuts
    spans = [(gathered + cut * width, gathered + (cut + 1) * width) for cut in range(cuts)]
    parts = [chip_product(away_rows, *span) for span in spans]
    crossed = [
        [to_chip(part[(step - 1) * rows : step * rows], step) for step in range(1, chips)]
        for part in parts
    ]
    parts, own_rows, far_rows = lax.optimization_barrier((parts, own_rows, far_rows))
    summed = [
        ((sum(arrived) + chip_product(own_rows, *span)) * inverse).astype(jnp.bfloat16)
        for arrived, span in zip(crossed, spans)
    ]

    ring = [[(own_index, w_far)]]
    ahead_w = behind_w = w_far
    for step in range(1, seg_count // 2 + 1):
        if step == 2:
            ahead_w, behind_w, ahead, behind = lax.optimization_barrier(
                (ahead_w, behind_w, ahead, behind)
            )
        if step == 3:
            ahead_w, behind_w, _ = lax.optimization_barrier((ahead_w, behind_w, mate))
        if step == 4:
            ahead_w, behind_w, _ = lax.optimization_barrier((ahead_w, behind_w, parts))
        ahead_w = lax.ppermute(ahead_w, "seg", forward)
        arrived = [(segment_at(own_place - step), ahead_w)]
        if step <= (seg_count - 1) // 2:
            behind_w = lax.ppermute(behind_w, "seg", backward)
            arrived.append((segment_at(own_place + step), behind_w))
        ring.append(arrived)
    ring[0:2] = [ring[0] + ring[1]]

    product = chip_product(own_rows, 0, gathered)
    left_own = [far_rows[:, 2 * features * i : 2 * features * i + features] for i in range(chips - 1)]
    left_mate = [far_rows[:, 2 * features * i + features : 2 * features * (i + 1)] for i in range(chips - 1)]
    left_own = jnp.concatenate(left_own, axis=1)
    left_mate = jnp.concatenate(left_mate, axis=1)
    placed = jnp.zeros((rows, gathered), jnp.float32)
    for arrived in ring:
        mine = jnp.concatenate([block for _, block in arrived], axis=1)
        other = to_core(mine)
        block = multiply(left_own, doubled(mine)) + multiply(left_mate, doubled(other))
        for place, (index, _) in enumerate(arrived):
            placed = lax.dynamic_update_slice_in_dim(
                placed, block[:, place * shard : (place + 1) * shard], index * shard, axis=1
            )
    first = ((product + placed) * inverse).astype(jnp.bfloat16)
    return jnp.concatenate([first] + summed, axis=1)


def solution(mesh):
    return jax.shard_map(
        per_device,
        mesh=mesh,
        in_specs=(
            P("seg", "head"),
            P("seg", "head"),
            P("seg", "head"),
            P("head", "seg"),
            P(),
            P("head"),
            P("head", None),
        ),
        out_specs=P(("seg", "head"), None),
        check_vma=False,
    )
```

```python
import jax
import jax.numpy as jnp
from jax import lax
from jax.sharding import PartitionSpec as P


def ring_order(count):
    half = (count + 1) // 2
    return [2 * i if i < half else 2 * (count - 1 - i) + 1 for i in range(count)]


def doubled(array):
    return (array * 2.0).astype(jnp.bfloat16)


def per_device(q_heads, k_heads, v_heads, log_decay, parent, norm_gain, w_out):
    segment_len, features = q_heads.shape
    head_count = log_decay.shape[0]
    head_width = features // head_count
    hidden = w_out.shape[1]
    seg_count = lax.axis_size("seg")
    head_parts = lax.axis_size("head")
    chips = head_parts // 2
    own_index = lax.axis_index("seg")
    own_head = lax.axis_index("head")
    own_chip, own_core = own_head // 2, own_head % 2
    rows = segment_len // head_parts

    swap = [(i, i ^ 1) for i in range(head_parts)]

    def to_core(array):
        return lax.ppermute(array, "head", swap)

    def to_chip(array, step):
        perm = [(i, (i + 2 * step) % head_parts) for i in range(head_parts)]
        return lax.ppermute(array, "head", perm)

    order = ring_order(seg_count)
    forward = [(order[i], order[(i + 1) % seg_count]) for i in range(seg_count)]
    backward = [(b, a) for a, b in forward]
    half = (seg_count + 1) // 2
    own_place = jnp.where(
        own_index % 2 == 0, own_index // 2, seg_count - 1 - own_index // 2
    )

    def segment_at(place):
        place = (place + seg_count) % seg_count
        return jnp.where(place < half, 2 * place, 2 * (seg_count - 1 - place) + 1)

    gathered = hidden * 2 // 3
    shard = gathered // seg_count
    w_piece = lax.dynamic_slice_in_dim(w_out, own_index * shard, shard, axis=1).astype(jnp.float32)
    w_piece, log_decay = lax.optimization_barrier((w_piece, log_decay))
    w_far = jnp.concatenate([to_chip(w_piece, step) for step in range(1, chips)], axis=0)
    gain_chip = jnp.concatenate([norm_gain, to_core(norm_gain)])
    gain_far = jnp.concatenate([to_chip(gain_chip, step) for step in range(1, chips)]) * 0.5
    gain_chip = gain_chip * jnp.repeat(jnp.array([1.0, 0.5], jnp.float32), norm_gain.shape[0])

    queries = q_heads.reshape(segment_len, head_count, head_width)
    key_rows = k_heads.reshape(segment_len, head_count, head_width)
    values = v_heads.reshape(segment_len, head_count, head_width)
    running = jnp.cumsum(log_decay, axis=1)
    segment_total = running[:, -1]
    key_weight = jnp.exp(segment_total[:, None] - running)
    weighted = key_rows.astype(jnp.float32) * key_weight.T[:, :, None]
    local_state = jnp.einsum(
        "shd,she->hde", weighted, values.astype(jnp.float32), precision=lax.Precision.HIGHEST
    )
    state_rows = head_count * head_width
    packed = jnp.concatenate(
        [
            local_state.reshape(state_rows, head_width),
            jnp.broadcast_to(segment_total[:, None], (head_count, head_width)),
        ],
        axis=0,
    )

    held = [(own_index, packed)]
    ahead = behind = packed
    for step in range(1, seg_count // 2 + 1):
        if step == 2:
            w_late, _ = lax.optimization_barrier((w_out, (ahead, behind)))
            ahead, behind, w_far = lax.optimization_barrier((ahead, behind, w_far))
            w_mate = to_core(w_late[:, gathered:].astype(jnp.float32))
        if step == 3:
            w_late, _ = lax.optimization_barrier((w_out, (ahead, behind)))
            w_mate_gathered = doubled(to_core(w_late[:, :gathered].astype(jnp.float32)))
        ahead = lax.ppermute(ahead, "seg", forward)
        held.append((segment_at(own_place - step), ahead))
        if step <= (seg_count - 1) // 2:
            behind = lax.ppermute(behind, "seg", backward)
            held.append((segment_at(own_place + step), behind))

    ahead, behind, w_mate = lax.optimization_barrier((ahead, behind, w_mate))
    held[-2 if seg_count % 2 else -1] = (held[-2 if seg_count % 2 else -1][0], ahead)
    w_mate = doubled(w_mate)

    scores = jnp.einsum("thd,shd->hts", queries, key_rows, preferred_element_type=jnp.float32)
    row_index = lax.broadcasted_iota(jnp.int32, (segment_len, segment_len), 0)
    col_index = lax.broadcasted_iota(jnp.int32, (segment_len, segment_len), 1)
    causal = row_index >= col_index
    log_gap = running[:, :, None] - running[:, None, :]
    decay_factor = jnp.where(causal[None], jnp.exp(jnp.minimum(log_gap, 0.0)), 0.0)
    weights = (scores * head_width ** (-0.5) * decay_factor).astype(jnp.bfloat16)
    within = jnp.einsum("hts,she->the", weights, values, preferred_element_type=jnp.float32)

    parent_id = parent[own_index]
    grand_id = jnp.where(parent_id >= 0, parent[jnp.maximum(parent_id, 0)], -1)
    parent_pack = sum(jnp.where(index == parent_id, pack, 0.0) for index, pack in held)
    grand_sum = sum(jnp.where(index == grand_id, pack[:state_rows], 0.0) for index, pack in held)
    shape = (head_count, head_width, head_width)
    prefix = jnp.exp(parent_pack[state_rows:])[:, None, :] * grand_sum.reshape(
        shape
    ) + parent_pack[:state_rows].reshape(shape)
    prefix_term = (
        jnp.einsum(
            "thd,hde->the", queries.astype(jnp.float32), prefix, precision=lax.Precision.HIGHEST
        )
        * jnp.exp(running).T[:, :, None]
    )
    attention = (prefix_term + within).reshape(segment_len, features)
    attention, w_mate = lax.optimization_barrier((attention, w_mate))

    attention = attention.reshape(chips, 2, rows, features)

    def core_rows(array, core):
        return lax.dynamic_index_in_dim(array, core, axis=1, keepdims=False)

    mate = to_core(core_rows(attention, 1 - own_core))
    chip_rows = jnp.concatenate([core_rows(attention, own_core), mate], axis=2)

    def chip_block(array, step):
        return lax.dynamic_index_in_dim(array, (own_chip + step) % chips, axis=0, keepdims=False)

    def scaled(array, gain):
        return (array * gain[None, :]).astype(jnp.bfloat16)

    own_wide = chip_block(chip_rows, 0)
    away = [chip_block(chip_rows, step) for step in range(1, chips)]
    far_wide = jnp.concatenate([to_chip(block, step) for step, block in enumerate(away, 1)], axis=1)
    own_rows = scaled(own_wide, gain_chip)
    away_rows = scaled(jnp.concatenate(away, axis=0), gain_chip)
    far_rows = scaled(far_wide, gain_far)
    total_squares = jnp.sum(own_wide * own_wide, axis=1) + jnp.sum(far_wide * far_wide, axis=1)
    inverse = (1.0 / jnp.sqrt(total_squares / (features * head_parts) + 1e-06))[:, None]

    def multiply(left, right):
        return jnp.dot(left, right, preferred_element_type=jnp.float32)

    def chip_product(left, low, high):
        mate_block = (
            w_mate_gathered[:, low:high]
            if high <= gathered
            else w_mate[:, low - gathered : high - gathered]
        )
        return multiply(left[:, :features], w_out[:, low:high]) + multiply(
            left[:, features:], mate_block
        )

    cuts = 2
    width = (hidden - gathered) // cuts
    spans = [(gathered + cut * width, gathered + (cut + 1) * width) for cut in range(cuts)]
    parts = [chip_product(away_rows, *span) for span in spans]
    crossed = [
        [to_chip(part[(step - 1) * rows : step * rows], step) for step in range(1, chips)]
        for part in parts
    ]
    parts, own_rows, far_rows = lax.optimization_barrier((parts, own_rows, far_rows))
    summed = [
        ((sum(arrived) + chip_product(own_rows, *span)) * inverse).astype(jnp.bfloat16)
        for arrived, span in zip(crossed, spans)
    ]

    ring = [[(own_index, w_far)]]
    ahead_w = behind_w = w_far
    for step in range(1, seg_count // 2 + 1):
        if step == 2:
            ahead_w, behind_w, ahead, behind = lax.optimization_barrier(
                (ahead_w, behind_w, ahead, behind)
            )
        if step == 3:
            ahead_w, behind_w, _ = lax.optimization_barrier((ahead_w, behind_w, mate))
        if step == 4:
            ahead_w, behind_w, _ = lax.optimization_barrier((ahead_w, behind_w, parts))
        ahead_w = lax.ppermute(ahead_w, "seg", forward)
        arrived = [(segment_at(own_place - step), ahead_w)]
        if step <= (seg_count - 1) // 2:
            behind_w = lax.ppermute(behind_w, "seg", backward)
            arrived.append((segment_at(own_place + step), behind_w))
        ring.append(arrived)
    ring[0:2] = [ring[0] + ring[1]]

    product = chip_product(own_rows, 0, gathered)
    left_own = [far_rows[:, 2 * features * i : 2 * features * i + features] for i in range(chips - 1)]
    left_mate = [far_rows[:, 2 * features * i + features : 2 * features * (i + 1)] for i in range(chips - 1)]
    left_own = jnp.concatenate(left_own, axis=1)
    left_mate = jnp.concatenate(left_mate, axis=1)
    placed = jnp.zeros((rows, gathered), jnp.float32)
    for arrived in ring:
        mine = jnp.concatenate([block for _, block in arrived], axis=1)
        other = to_core(mine)
        block = multiply(left_own, doubled(mine)) + multiply(left_mate, doubled(other))
        for place, (index, _) in enumerate(arrived):
            placed = lax.dynamic_update_slice_in_dim(
                placed, block[:, place * shard : (place + 1) * shard], index * shard, axis=1
            )
    first = ((product + placed) * inverse).astype(jnp.bfloat16)
    return jnp.concatenate([first] + summed, axis=1)


def solution(mesh):
    return jax.shard_map(
        per_device,
        mesh=mesh,
        in_specs=(
            P("seg", "head"),
            P("seg", "head"),
            P("seg", "head"),
            P("head", "seg"),
            P(),
            P("head"),
            P("head", None),
        ),
        out_specs=P(("seg", "head"), None),
        check_vma=False,
    )
```

```python
import jax
import jax.numpy as jnp
from jax import lax
from jax.sharding import PartitionSpec as P


def ring_order(count):
    half = (count + 1) // 2
    return [2 * i if i < half else 2 * (count - 1 - i) + 1 for i in range(count)]


def doubled(array):
    return (array * 2.0).astype(jnp.bfloat16)


def per_device(q_heads, k_heads, v_heads, log_decay, parent, norm_gain, w_out):
    segment_len, features = q_heads.shape
    head_count = log_decay.shape[0]
    head_width = features // head_count
    hidden = w_out.shape[1]
    seg_count = lax.axis_size("seg")
    head_parts = lax.axis_size("head")
    chips = head_parts // 2
    own_index = lax.axis_index("seg")
    own_head = lax.axis_index("head")
    own_chip, own_core = own_head // 2, own_head % 2
    rows = segment_len // head_parts

    swap = [(i, i ^ 1) for i in range(head_parts)]

    def to_core(array):
        return lax.ppermute(array, "head", swap)

    def to_chip(array, step):
        perm = [(i, (i + 2 * step) % head_parts) for i in range(head_parts)]
        return lax.ppermute(array, "head", perm)

    order = ring_order(seg_count)
    forward = [(order[i], order[(i + 1) % seg_count]) for i in range(seg_count)]
    backward = [(b, a) for a, b in forward]
    half = (seg_count + 1) // 2
    own_place = jnp.where(
        own_index % 2 == 0, own_index // 2, seg_count - 1 - own_index // 2
    )

    def segment_at(place):
        place = (place + seg_count) % seg_count
        return jnp.where(place < half, 2 * place, 2 * (seg_count - 1 - place) + 1)

    gathered = hidden // 2
    shard = gathered // seg_count
    w_piece = lax.dynamic_slice_in_dim(w_out, own_index * shard, shard, axis=1).astype(jnp.float32)
    w_piece, log_decay = lax.optimization_barrier((w_piece, log_decay))
    w_far = jnp.concatenate([to_chip(w_piece, step) for step in range(1, chips)], axis=0)
    gain_chip = jnp.concatenate([norm_gain, to_core(norm_gain)])
    gain_far = jnp.concatenate([to_chip(gain_chip, step) for step in range(1, chips)]) * 0.5
    gain_chip = gain_chip * jnp.repeat(jnp.array([1.0, 0.5], jnp.float32), norm_gain.shape[0])

    queries = q_heads.reshape(segment_len, head_count, head_width)
    key_rows = k_heads.reshape(segment_len, head_count, head_width)
    values = v_heads.reshape(segment_len, head_count, head_width)
    running = jnp.cumsum(log_decay, axis=1)
    segment_total = running[:, -1]
    key_weight = jnp.exp(segment_total[:, None] - running)
    weighted = key_rows.astype(jnp.float32) * key_weight.T[:, :, None]
    local_state = jnp.einsum(
        "shd,she->hde", weighted, values.astype(jnp.float32), precision=lax.Precision.HIGHEST
    )
    state_rows = head_count * head_width
    packed = jnp.concatenate(
        [
            local_state.reshape(state_rows, head_width),
            jnp.broadcast_to(segment_total[:, None], (head_count, head_width)),
        ],
        axis=0,
    )

    w_late, packed = lax.optimization_barrier((w_out, packed))
    w_mate = to_core(w_late[:, gathered:].astype(jnp.float32))

    held = [(own_index, packed)]
    ahead = behind = packed
    for step in range(1, seg_count // 2 + 1):
        if step == 2:
            ahead, behind, w_far = lax.optimization_barrier((ahead, behind, w_far))
        if step == 3:
            w_late, _ = lax.optimization_barrier((w_out, (ahead, behind)))
            w_mate_gathered = doubled(to_core(w_late[:, :gathered].astype(jnp.float32)))
        ahead = lax.ppermute(ahead, "seg", forward)
        held.append((segment_at(own_place - step), ahead))
        if step <= (seg_count - 1) // 2:
            behind = lax.ppermute(behind, "seg", backward)
            held.append((segment_at(own_place + step), behind))

    ahead, behind, w_mate = lax.optimization_barrier((ahead, behind, w_mate))
    held[-2 if seg_count % 2 else -1] = (held[-2 if seg_count % 2 else -1][0], ahead)
    w_mate = doubled(w_mate)

    scores = jnp.einsum("thd,shd->hts", queries, key_rows, preferred_element_type=jnp.float32)
    row_index = lax.broadcasted_iota(jnp.int32, (segment_len, segment_len), 0)
    col_index = lax.broadcasted_iota(jnp.int32, (segment_len, segment_len), 1)
    causal = row_index >= col_index
    log_gap = running[:, :, None] - running[:, None, :]
    decay_factor = jnp.where(causal[None], jnp.exp(jnp.minimum(log_gap, 0.0)), 0.0)
    weights = (scores * head_width ** (-0.5) * decay_factor).astype(jnp.bfloat16)
    within = jnp.einsum("hts,she->the", weights, values, preferred_element_type=jnp.float32)

    parent_id = parent[own_index]
    grand_id = jnp.where(parent_id >= 0, parent[jnp.maximum(parent_id, 0)], -1)
    parent_pack = sum(jnp.where(index == parent_id, pack, 0.0) for index, pack in held)
    grand_sum = sum(jnp.where(index == grand_id, pack[:state_rows], 0.0) for index, pack in held)
    shape = (head_count, head_width, head_width)
    prefix = jnp.exp(parent_pack[state_rows:])[:, None, :] * grand_sum.reshape(
        shape
    ) + parent_pack[:state_rows].reshape(shape)
    prefix_term = (
        jnp.einsum(
            "thd,hde->the", queries.astype(jnp.float32), prefix, precision=lax.Precision.HIGHEST
        )
        * jnp.exp(running).T[:, :, None]
    )
    attention = (prefix_term + within).reshape(segment_len, features)
    attention, w_mate = lax.optimization_barrier((attention, w_mate))

    attention = attention.reshape(chips, 2, rows, features)

    def core_rows(array, core):
        return lax.dynamic_index_in_dim(array, core, axis=1, keepdims=False)

    mate = to_core(core_rows(attention, 1 - own_core))
    chip_rows = jnp.concatenate([core_rows(attention, own_core), mate], axis=2)

    def chip_block(array, step):
        return lax.dynamic_index_in_dim(array, (own_chip + step) % chips, axis=0, keepdims=False)

    def scaled(array, gain):
        return (array * gain[None, :]).astype(jnp.bfloat16)

    own_wide = chip_block(chip_rows, 0)
    away = [chip_block(chip_rows, step) for step in range(1, chips)]
    far_wide = jnp.concatenate([to_chip(block, step) for step, block in enumerate(away, 1)], axis=1)
    own_rows = scaled(own_wide, gain_chip)
    away_rows = scaled(jnp.concatenate(away, axis=0), gain_chip)
    far_rows = scaled(far_wide, gain_far)
    total_squares = jnp.sum(own_wide * own_wide, axis=1) + jnp.sum(far_wide * far_wide, axis=1)
    inverse = (1.0 / jnp.sqrt(total_squares / (features * head_parts) + 1e-06))[:, None]

    def multiply(left, right):
        return jnp.dot(left, right, preferred_element_type=jnp.float32)

    def chip_product(left, low, high):
        mate_block = (
            w_mate_gathered[:, low:high]
            if high <= gathered
            else w_mate[:, low - gathered : high - gathered]
        )
        return multiply(left[:, :features], w_out[:, low:high]) + multiply(
            left[:, features:], mate_block
        )

    cuts = 3
    width = (hidden - gathered) // cuts
    spans = [(gathered + cut * width, gathered + (cut + 1) * width) for cut in range(cuts)]
    parts = [chip_product(away_rows, *span) for span in spans]
    crossed = [
        [to_chip(part[(step - 1) * rows : step * rows], step) for step in range(1, chips)]
        for part in parts
    ]
    parts, own_rows, far_rows = lax.optimization_barrier((parts, own_rows, far_rows))
    summed = [
        ((sum(arrived) + chip_product(own_rows, *span)) * inverse).astype(jnp.bfloat16)
        for arrived, span in zip(crossed, spans)
    ]

    ring = [[(own_index, w_far)]]
    ahead_w = behind_w = w_far
    for step in range(1, seg_count // 2 + 1):
        if step == 2:
            ahead_w, behind_w, ahead, behind = lax.optimization_barrier(
                (ahead_w, behind_w, ahead, behind)
            )
        if step == 3:
            ahead_w, behind_w, _ = lax.optimization_barrier((ahead_w, behind_w, mate))
        if step == 4:
            ahead_w, behind_w, _ = lax.optimization_barrier((ahead_w, behind_w, parts))
        ahead_w = lax.ppermute(ahead_w, "seg", forward)
        arrived = [(segment_at(own_place - step), ahead_w)]
        if step <= (seg_count - 1) // 2:
            behind_w = lax.ppermute(behind_w, "seg", backward)
            arrived.append((segment_at(own_place + step), behind_w))
        ring.append(arrived)
    ring[0:2] = [ring[0] + ring[1]]

    product = chip_product(own_rows, 0, gathered)
    left_own = [far_rows[:, 2 * features * i : 2 * features * i + features] for i in range(chips - 1)]
    left_mate = [far_rows[:, 2 * features * i + features : 2 * features * (i + 1)] for i in range(chips - 1)]
    left_own = jnp.concatenate(left_own, axis=1)
    left_mate = jnp.concatenate(left_mate, axis=1)
    placed = jnp.zeros((rows, gathered), jnp.float32)
    for arrived in ring:
        mine = jnp.concatenate([block for _, block in arrived], axis=1)
        other = to_core(mine)
        block = multiply(left_own, doubled(mine)) + multiply(left_mate, doubled(other))
        for place, (index, _) in enumerate(arrived):
            placed = lax.dynamic_update_slice_in_dim(
                placed, block[:, place * shard : (place + 1) * shard], index * shard, axis=1
            )
    first = ((product + placed) * inverse).astype(jnp.bfloat16)
    return jnp.concatenate([first] + summed, axis=1)


def solution(mesh):
    return jax.shard_map(
        per_device,
        mesh=mesh,
        in_specs=(
            P("seg", "head"),
            P("seg", "head"),
            P("seg", "head"),
            P("head", "seg"),
            P(),
            P("head"),
            P("head", None),
        ),
        out_specs=P(("seg", "head"), None),
        check_vma=False,
    )
```
